128 devices in a mesh: frame: 8 (over y, z_hi), strip: 16 (over z_lo, x, core).
Axes of the slice: x: 4, y: 4, z: 4 (z_hi: 2, z_lo: 2; z = z_hi * 2 + z_lo), core: 2. Of those that a mesh axis runs over, the one named last changes fastest.
Arguments:
- queries: bfloat16 [32, 1024, 3072], P('frame', 'strip'), may hold values from -96 to 96
- key_states: bfloat16 [32, 1024, 3072], P('frame', 'strip'), may hold values from -4 to 4
- value_states: bfloat16 [32, 1024, 3072], P('frame', 'strip'), may hold values from -6 to 6
- block_masks: int32 [4, 8, 8], replicated, may hold values from 0 to 1, as said below
- head_pattern: int32 [16], replicated, may hold values from 0 to 3
Outputs:
- attended: bfloat16 [32, 1024, 3072], P('frame', 'strip')
The draws below stay inside these ranges and needn't reach their ends.
Inputs may be any that keep to these rules, and one draw needn't show every extreme that they name: Every pattern reads its diagonal block pairs: block_masks[p, b, b] = 1 for all p and b.
All inputs are finite; a program needn't handle non-finite values.
Results may differ from the reference program's by a relative error of at most 0.0046.
Values may be sent and summed in bfloat16 or wider, within the bound.
No kernel may reach another device: no remote copies, remote signals or barrier semaphores. Data moves between devices by JAX's collectives and lax.ppermute only.
A program may use at most 192 MiB of HBM per device.

```python
import math
import jax
import jax.numpy as jnp
from jax import lax

DH = 128
HS = 16
HT = 8
BLK = 128
NPAT = 4
SP_DEV = 64
FRAMES = 32
SPOTS = 1024
BLOCKS = 8
CHANNELS = 3072
N_STRIP = 16


def paired_draw(key):
    base_key = jax.random.fold_in(key, 11)
    first_key, second_key = jax.random.split(base_key, 2)
    full_shape = (FRAMES, SPOTS, CHANNELS)
    keys_drawn = jnp.clip(jax.random.normal(first_key, full_shape, jnp.float32), -4.0, 4.0)
    queries_drawn = jnp.clip(jax.random.normal(second_key, full_shape, jnp.float32), -4.0, 4.0)
    return (queries_drawn, keys_drawn)


def draw_queries(key, part):
    return paired_draw(key)[0].astype(jnp.bfloat16)


def draw_key_states(key, part):
    return paired_draw(key)[1].astype(jnp.bfloat16)


def draw_block_masks(key, part):
    level_key, toss_key = jax.random.split(jax.random.fold_in(key, 23))
    levels = jax.random.randint(level_key, (NPAT, 1, 1), 1, 4)
    tosses = jax.random.randint(toss_key, (NPAT, BLOCKS, BLOCKS), 0, 4)
    diagonal = jnp.arange(BLOCKS)[:, None] == jnp.arange(BLOCKS)[None, :]
    return jnp.where(diagonal[None] | (tosses < levels), 1, 0).astype(jnp.int32)


def plant(result, rng, low, top_value):
    index_at = [jax.random.randint(jax.random.fold_in(rng, axis), (), 0, length) for axis, length in enumerate(result.shape)]
    widest = result.shape.index(max(result.shape))
    next_to = index_at[:widest] + [(index_at[widest] + 1) % result.shape[widest]] + index_at[widest + 1:]
    return result.at[tuple(index_at)].set(low).at[tuple(next_to)].set(top_value)


def level_of(rng, shape, shards, least, top_value):
    level = 1.0
    for axis_at, parts in shards:
        heights = jax.random.uniform(jax.random.fold_in(jax.random.fold_in(rng, 6), axis_at), (parts,), jnp.float32, least / len(shards), top_value / len(shards))
        level = level * jnp.repeat(jnp.exp(heights), shape[axis_at] // parts).reshape((-1,) + (1,) * (len(shape) - 1 - axis_at))
    return level


def gaussian(own_key, extent, spread, bound, cuts=(), held_as=jnp.bfloat16):
    result = spread * jax.random.normal(own_key, extent, jnp.float32)
    if cuts:
        result = result * level_of(own_key, extent, cuts, -0.22, 0.18)
    return jnp.clip(result, -bound, bound).astype(held_as)


def setup_inputs(seed: int = 0) -> dict:
    key_list = jax.random.split(jax.random.key(seed), 6)
    queries = draw_queries(jax.random.fold_in(key_list[5], 71), 0)
    key_states = draw_key_states(jax.random.fold_in(key_list[5], 71), 0)
    value_states = gaussian(key_list[2], (FRAMES, SPOTS, CHANNELS), 1.0, 6.0, ((0, 8), (1, 16)))
    block_masks = draw_block_masks(jax.random.fold_in(key_list[5], 71), 0)
    head_pattern = plant(jax.random.randint(key_list[4], (HS,), 0, NPAT), jax.random.fold_in(key_list[4], 1), 0, NPAT - 1).astype(jnp.int32)
    return {"queries": queries, "key_states": key_states, "value_states": value_states, "block_masks": block_masks, "head_pattern": head_pattern}


NEG_FILL = -1e+30

def attend(query_rows, key_rows, value_rows, allowed):
    scores = jnp.dot(query_rows, key_rows.T, preferred_element_type=jnp.float32) * (1.0 / math.sqrt(DH))
    scores = jnp.where(allowed, scores, NEG_FILL)
    highest = lax.optimization_barrier(jnp.max(scores, axis=-1, keepdims=True))
    weights = jnp.where(allowed, jnp.exp(scores - highest), 0.0)
    totals = lax.optimization_barrier(jnp.sum(weights, axis=-1, keepdims=True))
    mixed = jnp.dot(weights.astype(jnp.bfloat16), value_rows, preferred_element_type=jnp.float32)
    return (mixed / totals).astype(jnp.bfloat16)

def reference(queries, key_states, value_states, block_masks, head_pattern):
    block_of = jnp.arange(SPOTS) // BLK
    pieces = []
    for head in range(HS):
        first = head * DH
        pattern = block_masks[head_pattern[head]]
        allowed = pattern[block_of][:, block_of] > 0

        def per_frame(inputs, allowed=allowed):
            return attend(inputs[0], inputs[1], inputs[2], allowed)
        pieces.append(lax.map(per_frame, (queries[:, :, first:first + DH], key_states[:, :, first:first + DH], value_states[:, :, first:first + DH])))
    strip_of = jnp.arange(5 * SP_DEV) // SP_DEV
    for head in range(HT):
        first = (HS + head) * DH
        query_head = queries[:, :, first:first + DH]
        keys_padded = jnp.pad(key_states[:, :, first:first + DH], ((0, 0), (2 * SP_DEV, 2 * SP_DEV), (0, 0)))
        values_padded = jnp.pad(value_states[:, :, first:first + DH], ((0, 0), (2 * SP_DEV, 2 * SP_DEV), (0, 0)))

        def per_group(group, query_head=query_head, keys_padded=keys_padded, values_padded=values_padded):
            begin = (group * SP_DEV).astype(jnp.int32)
            query_rows = lax.dynamic_slice_in_dim(query_head, begin, SP_DEV, 1).reshape(FRAMES * SP_DEV, DH)
            key_rows = lax.dynamic_slice_in_dim(keys_padded, begin, 5 * SP_DEV, 1).reshape(FRAMES * 5 * SP_DEV, DH)
            value_rows = lax.dynamic_slice_in_dim(values_padded, begin, 5 * SP_DEV, 1).reshape(FRAMES * 5 * SP_DEV, DH)
            neighbour = group - 2 + strip_of
            usable = (neighbour >= 0) & (neighbour < N_STRIP)
            allowed = jnp.broadcast_to(jnp.tile(usable, FRAMES)[None, :], (FRAMES * SP_DEV, FRAMES * 5 * SP_DEV))
            return attend(query_rows, key_rows, value_rows, allowed).reshape(FRAMES, SP_DEV, DH)
        stacked = lax.map(per_group, jnp.arange(N_STRIP, dtype=jnp.int32))
        pieces.append(stacked.transpose(1, 0, 2, 3).reshape(FRAMES, SPOTS, DH))
    return jnp.concatenate(pieces, axis=-1)
```

```python
import math

import jax
import jax.numpy as jnp
from jax import lax
from jax.experimental import pallas as pl
from jax.experimental.pallas import tpu as pltpu
from jax.sharding import PartitionSpec as P

DH = 128
HS = 16
HT = 8
BLK = 128
NF = 8
NS = 16

NEG_FILL = -1e30
RATE = math.log2(math.e) / math.sqrt(DH)


BF16 = jnp.bfloat16
F32 = jnp.float32


def whole():
    return pl.BlockSpec(memory_space=pltpu.VMEM)


def scalars():
    return pl.BlockSpec(memory_space=pltpu.SMEM)


def params(**kw):
    return pltpu.CompilerParams(vmem_limit_bytes=56 * 1024 * 1024, **kw)


def anywhere():
    return pl.BlockSpec(memory_space=pl.ANY)


def split_spatial_kernel(q_ref, k_ref, v_ref, out_ref, slab_ref, in_sem, out_sem):
    arrive = []
    for head in range(HS):
        for part, ref in enumerate((q_ref, k_ref, v_ref)):
            arrive.append(
                pltpu.make_async_copy(
                    ref.at[:, :, head * DH : (head + 1) * DH],
                    slab_ref.at[head, part],
                    in_sem.at[len(arrive)],
                )
            )
            arrive[-1].start()
    leave = []
    for head in range(HS):
        for part in range(3):
            arrive[3 * head + part].wait()
        leave.append(pltpu.make_async_copy(slab_ref.at[head], out_ref.at[head], out_sem.at[head]))
        leave[-1].start()
    for copy in leave:
        copy.wait()


def split_spatial(queries, keys, values):
    frames, spots, _ = queries.shape
    shape = (HS, 3, frames, spots, DH)
    return pl.pallas_call(
        split_spatial_kernel,
        in_specs=[anywhere()] * 3,
        out_specs=anywhere(),
        out_shape=jax.ShapeDtypeStruct(shape, BF16),
        scratch_shapes=[
            pltpu.VMEM(shape, BF16),
            pltpu.SemaphoreType.DMA((HS * 3,)),
            pltpu.SemaphoreType.DMA((HS,)),
        ],
        compiler_params=params(),
        name="split_spatial",
    )(queries, keys, values)


def split_temporal_kernel(group_ref, q_ref, k_ref, v_ref, *rest):
    out_refs, (slab_ref, in_sem, out_sem) = rest[:NF], rest[NF:]
    group = group_ref[0]
    arrive = []
    for slot in range(NF):
        at = pl.multiple_of((HS + lax.rem(group + slot, NF)) * DH, DH)
        for part, ref in enumerate((q_ref, k_ref, v_ref)):
            arrive.append(
                pltpu.make_async_copy(
                    ref.at[:, :, pl.ds(at, DH)], slab_ref.at[slot, part], in_sem.at[len(arrive)]
                )
            )
            arrive[-1].start()
    leave = []
    for slot in range(NF):
        for part in range(3):
            arrive[3 * slot + part].wait()
        leave.append(pltpu.make_async_copy(slab_ref.at[slot], out_refs[slot], out_sem.at[slot]))
        leave[-1].start()
    for copy in leave:
        copy.wait()


def split_temporal(group, queries, keys, values):
    frames, spots, _ = queries.shape
    shape = (3, frames, spots, DH)
    return pl.pallas_call(
        split_temporal_kernel,
        in_specs=[scalars()] + [anywhere()] * 3,
        out_specs=[anywhere()] * NF,
        out_shape=[jax.ShapeDtypeStruct(shape, BF16)] * NF,
        scratch_shapes=[
            pltpu.VMEM((NF, *shape), BF16),
            pltpu.SemaphoreType.DMA((NF * 3,)),
            pltpu.SemaphoreType.DMA((NF,)),
        ],
        compiler_params=params(),
        name="split_temporal",
    )(group, queries, keys, values)


def collect_kernel(*refs):
    slabs, (q_ref, kv_ref, q_buf, kv_buf, in_sem, out_sem) = refs[:NF], refs[NF:]
    arrive = []
    for slot in range(NF):
        arrive.append(pltpu.make_async_copy(slabs[slot].at[0], q_buf.at[slot], in_sem.at[2 * slot]))
        arrive[-1].start()
        arrive.append(
            pltpu.make_async_copy(
                slabs[slot].at[1:3], kv_buf.at[:, slot], in_sem.at[2 * slot + 1]
            )
        )
        arrive[-1].start()
    for copy in arrive:
        copy.wait()
    leave = [
        pltpu.make_async_copy(q_buf, q_ref, out_sem.at[0]),
        pltpu.make_async_copy(kv_buf, kv_ref, out_sem.at[1]),
    ]
    for copy in leave:
        copy.start()
    for copy in leave:
        copy.wait()


def collect(slabs):
    _, frames, spots, _ = slabs[0].shape
    q_shape = (NF, frames, spots, DH)
    kv_shape = (2, NF, frames, spots, DH)
    return pl.pallas_call(
        collect_kernel,
        in_specs=[anywhere()] * NF,
        out_specs=[anywhere()] * 2,
        out_shape=[jax.ShapeDtypeStruct(q_shape, BF16), jax.ShapeDtypeStruct(kv_shape, BF16)],
        scratch_shapes=[
            pltpu.VMEM(q_shape, BF16),
            pltpu.VMEM(kv_shape, BF16),
            pltpu.SemaphoreType.DMA((2 * NF,)),
            pltpu.SemaphoreType.DMA((2,)),
        ],
        compiler_params=params(),
        name="collect",
    )(*slabs)


QT = 512
QS = 256


def scores_of(q, k):
    return lax.dot_general(q, k, (((1,), (1,)), ((), ())), preferred_element_type=F32)


def temporal_kernel(count, resume, finish, *refs):
    use_ref, q_ref = refs[:2]
    kv_refs = refs[2 : 2 + count]
    rest = list(refs[2 + count :])
    if resume:
        old_top, old_mix = rest[:2]
        rest = rest[2:]
    if finish:
        group_ref = rest.pop(0)
        out_ref, top_ref, mix_ref, k_buf, v_buf, s_buf, sem = rest
    else:
        top_ref, mix_ref, k_buf, v_buf, s_buf, sem = rest
    rows = k_buf.shape[1]
    tiles = rows // QT

    def copies(index):
        return (
            pltpu.make_async_copy(kv_refs[index].at[0], k_buf.at[index], sem.at[2 * index]),
            pltpu.make_async_copy(
                kv_refs[index].at[1], v_buf.at[index, :, 0:DH], sem.at[2 * index + 1]
            ),
        )

    for index in range(count):
        for copy in copies(index):
            copy.start()
    for index in range(count):
        v_buf[index, :, DH:] = jnp.ones((rows, DH), BF16)
    if resume:
        top_ref[...] = old_top[...]
        mix_ref[...] = old_mix[...]
    else:
        top_ref[...] = jnp.full(top_ref.shape, NEG_FILL, F32)
        mix_ref[...] = jnp.zeros(mix_ref.shape, F32)
    for index in range(count):
        for copy in copies(index):
            copy.wait()

    def strip(index, carry):
        @pl.when(use_ref[index] > 0)
        def _():
            k = k_buf[index]

            def q_tile(i):
                return q_ref[i * QT : (i + 1) * QT]

            s_buf[0] = scores_of(q_tile(0), k)
            for i in range(tiles):
                if i + 1 < tiles:
                    s_buf[(i + 1) % 2] = scores_of(q_tile(i + 1), k)
                at = slice(i * QT, (i + 1) * QT)
                s = s_buf[i % 2]
                before = top_ref[at]
                top = jnp.maximum(before, jnp.max(s, axis=1, keepdims=True))
                fade = jnp.exp2((before - top) * RATE)
                weights = jnp.exp2((s - top[:, :1]) * RATE).astype(BF16)
                mixed = jnp.dot(weights, v_buf[index], preferred_element_type=F32)
                mix_ref[at] = mixed + mix_ref[at] * jnp.concatenate([fade, fade], axis=1)
                top_ref[at] = top

        return carry

    lax.fori_loop(0, count, strip, 0)
    if finish:
        group = group_ref[0]
        slots = out_ref.shape[0]
        per = rows // slots
        for i in range(slots):
            at = slice(i * per, (i + 1) * per)
            target = lax.rem(group + (slots - i), slots)
            out_ref[target] = (mix_ref[at, :DH] / mix_ref[at, DH:]).astype(BF16)


def temporal(use, q, strips, state=None, group=None):
    rows = q.shape[0]
    count = len(strips)
    state_shape = [
        jax.ShapeDtypeStruct((rows, DH), F32),
        jax.ShapeDtypeStruct((rows, 2 * DH), F32),
    ]
    args = [use, q, *strips]
    in_specs = [scalars(), whole(), *[anywhere()] * count]
    scratch = [
        pltpu.VMEM((count, rows, DH), BF16),
        pltpu.VMEM((count, rows, 2 * DH), BF16),
        pltpu.VMEM((2, QT, rows), F32),
        pltpu.SemaphoreType.DMA((2 * count,)),
    ]
    if state is not None:
        args += list(state)
        in_specs += [whole()] * 2
    if group is not None:
        args.append(group)
        in_specs.append(scalars())
        out_shape = jax.ShapeDtypeStruct((NF, rows // NF, DH), BF16)
        out_specs = whole()
        scratch = [pltpu.VMEM(s.shape, s.dtype) for s in state_shape] + scratch
    else:
        out_shape = state_shape
        out_specs = [whole()] * 2
    cost = pl.CostEstimate(
        flops=count * rows**2 * DH * 8,
        transcendentals=count * rows**2,
        bytes_accessed=count * rows * DH * 4,
    )
    return pl.pallas_call(
        lambda *refs: temporal_kernel(count, state is not None, group is not None, *refs),
        in_specs=in_specs,
        out_specs=out_specs,
        out_shape=out_shape,
        scratch_shapes=scratch,
        compiler_params=params(),
        cost_estimate=cost,
        name="temporal_last" if group is not None else "temporal_first",
    )(*args)


def spatial_kernel(strip_ref, pattern_ref, mask_ref, qkv_ref, out_ref, q_buf, k_buf, v_buf, s_buf, sem):
    pattern = pattern_ref[strip_ref[0]]
    strips, frames, spots, _ = out_ref.shape
    positions = strips * spots
    blocks = positions // BLK
    tiles = positions // QS
    per = QS // spots
    copies = []
    for f in range(frames):
        for part, buf in enumerate((q_buf, k_buf, v_buf)):
            target = buf.at[f, :, :, 0:DH] if part == 2 else buf.at[f]
            copies.append(
                pltpu.make_async_copy(qkv_ref.at[:, part, f], target, sem.at[len(copies)])
            )
            copies[-1].start()
    v_buf[:, :, :, DH:] = jnp.ones((frames, strips, spots, DH), BF16)
    for copy in copies:
        copy.wait()

    def raw(f, i):
        q = q_buf[f, i * per : (i + 1) * per].reshape(QS, DH)
        return scores_of(q, k_buf[f].reshape(positions, DH))

    def masked(s, i):
        rows = []
        for r in range(QS // BLK):
            row = (pattern * blocks + i * (QS // BLK) + r) * blocks
            cells = []
            for j in range(blocks):
                bias = jnp.where(mask_ref[row + j] > 0, 0.0, NEG_FILL)
                cells.append(s[r * BLK : (r + 1) * BLK, j * BLK : (j + 1) * BLK] + bias)
            rows.append(jnp.concatenate(cells, axis=1))
        return jnp.concatenate(rows, axis=0)

    s_buf[0] = raw(0, 0)

    def frame(f, carry):
        v = v_buf[f].reshape(positions, 2 * DH)
        for i in range(tiles):
            if i + 1 < tiles:
                s_buf[(i + 1) % 2] = raw(f, i + 1)
            else:
                s_buf[(i + 1) % 2] = raw(jnp.minimum(f + 1, frames - 1), 0)
            s = masked(s_buf[i % 2], i)
            top = jnp.max(s, axis=1, keepdims=True)
            weights = jnp.exp2((s - top) * RATE).astype(BF16)
            mixed = jnp.dot(weights, v, preferred_element_type=F32)
            result = (mixed[:, :DH] / mixed[:, DH:]).astype(BF16)
            out_ref[i * per : (i + 1) * per, f] = result.reshape(per, spots, DH)
        return carry

    lax.fori_loop(0, frames, frame, 0)


def spatial(strip, head_pattern, masks, qkv):
    strips, _, frames, spots, _ = qkv.shape
    positions = strips * spots
    cost = pl.CostEstimate(
        flops=frames * positions**2 * DH * 8,
        transcendentals=frames * positions**2,
        bytes_accessed=4 * strips * frames * spots * DH * 2,
    )
    return pl.pallas_call(
        spatial_kernel,
        in_specs=[scalars()] * 3 + [anywhere()],
        out_specs=whole(),
        scratch_shapes=[
            pltpu.VMEM((frames, strips, spots, DH), BF16),
            pltpu.VMEM((frames, strips, spots, DH), BF16),
            pltpu.VMEM((frames, strips, spots, 2 * DH), BF16),
            pltpu.VMEM((2, QS, positions), F32),
            pltpu.SemaphoreType.DMA((3 * frames,)),
        ],
        out_shape=jax.ShapeDtypeStruct((strips, frames, spots, DH), BF16),
        compiler_params=params(),
        cost_estimate=cost,
        name="spatial",
    )(strip, head_pattern, masks, qkv)


def join_kernel(first, count, heads_ref, *rest):
    out_ref, slab_ref, in_sem, out_sem = rest[-4:]
    arrive = []
    for head in range(count):
        arrive.append(pltpu.make_async_copy(heads_ref.at[head], slab_ref.at[head], in_sem.at[head]))
        arrive[-1].start()
    leave = []
    for head in range(count):
        arrive[head].wait()
        at = (first + head) * DH
        leave.append(
            pltpu.make_async_copy(
                slab_ref.at[head], out_ref.at[:, :, at : at + DH], out_sem.at[head]
            )
        )
        leave[-1].start()
    for copy in leave:
        copy.wait()


def join(heads, first, partial=None):
    count, frames, spots, _ = heads.shape
    shape = (frames, spots, (HS + HT) * DH)
    return pl.pallas_call(
        lambda *refs: join_kernel(first, count, *refs),
        in_specs=[anywhere()] * (1 if partial is None else 2),
        out_specs=anywhere(),
        out_shape=jax.ShapeDtypeStruct(shape, BF16),
        scratch_shapes=[
            pltpu.VMEM(heads.shape, BF16),
            pltpu.SemaphoreType.DMA((count,)),
            pltpu.SemaphoreType.DMA((count,)),
        ],
        input_output_aliases={} if partial is None else {1: 0},
        compiler_params=params(),
        name="join_spatial" if partial is None else "join_temporal",
    )(*([heads] if partial is None else [heads, partial]))


def body(queries, keys, values, block_masks, head_pattern):
    frames, spots, _ = queries.shape
    rows = NF * frames * spots
    group = lax.axis_index("frame").astype(jnp.int32)
    strip = lax.axis_index("strip").astype(jnp.int32)

    slabs = split_temporal(group.reshape(1), queries, keys, values)
    slabs = [slabs[0]] + [
        lax.ppermute(slabs[d], "frame", [(i, (i + d) % NF) for i in range(NF)])
        for d in range(1, NF)
    ]
    qkv = split_spatial(queries, keys, values)
    qkv = lax.all_to_all(qkv, "strip", split_axis=0, concat_axis=0, tiled=True)
    t_q, own = collect(slabs)
    t_q = t_q.reshape(rows, DH)
    own = own.reshape(2, rows, DH)

    swap = [(i, i ^ 1) for i in range(NS)]
    shared_from = [i + 2 if i % 2 == 0 else i - 2 for i in range(NS)]
    single_from = [i - 2 if i % 2 == 0 else i + 2 for i in range(NS)]
    shared = lax.ppermute(own, "strip", [(s, i) for i, s in enumerate(shared_from) if 0 <= s < NS])
    single = lax.ppermute(own, "strip", [(s, i) for i, s in enumerate(single_from) if 0 <= s < NS])
    partner = lax.ppermute(own, "strip", swap)
    passed = lax.ppermute(shared, "strip", swap)

    step = 1 - 2 * lax.rem(strip, 2)
    sources = strip + jnp.array([2, -2, -1], jnp.int32) * step
    use = ((sources >= 0) & (sources < NS)).astype(jnp.int32)

    state = temporal(jnp.ones((2,), jnp.int32), t_q, [own, partner])
    t_out = temporal(use, t_q, [shared, single, passed], state, group.reshape(1))

    s_out = spatial(strip.reshape(1), head_pattern, block_masks.reshape(-1), qkv)
    s_out = lax.all_to_all(s_out, "strip", split_axis=0, concat_axis=0, tiled=True)
    partial = join(s_out, 0)

    t_out = t_out.reshape(NF, frames, spots, DH)
    t_out = lax.all_to_all(t_out, "frame", split_axis=0, concat_axis=0, tiled=True)
    return join(t_out, HS, partial)


def solution(mesh):
    spec = P("frame", "strip", None)
    return jax.shard_map(
        body,
        mesh=mesh,
        in_specs=(spec, spec, spec, P(), P()),
        out_specs=spec,
        check_vma=False,
    )
```

```python
import math

import jax
import jax.numpy as jnp
from jax import lax
from jax.experimental import pallas as pl
from jax.experimental.pallas import tpu as pltpu
from jax.sharding import PartitionSpec as P


DH = 128
HS = 16
HT = 8
BLK = 128
NF = 8
NS = 16
QT = 512
QS = 256

NEG_FILL = -1e30
RATE = math.log2(math.e) / math.sqrt(DH)


BF16 = jnp.bfloat16
F32 = jnp.float32


def whole():
    return pl.BlockSpec(memory_space=pltpu.VMEM)


def scalars():
    return pl.BlockSpec(memory_space=pltpu.SMEM)


def anywhere():
    return pl.BlockSpec(memory_space=pl.ANY)


def in_vmem(block):
    return pltpu.with_memory_space_constraint(block, pltpu.VMEM)


def in_hbm(block):
    return pltpu.with_memory_space_constraint(block, pltpu.HBM)


def params(mib=8):
    return pltpu.CompilerParams(vmem_limit_bytes=mib * 1024 * 1024)


def split_spatial_kernel(q_ref, k_ref, v_ref, out_ref, sem):
    copies = []
    for head in range(HS):
        for part, ref in enumerate((q_ref, k_ref, v_ref)):
            copies.append(
                pltpu.make_async_copy(
                    ref.at[:, :, head * DH : (head + 1) * DH],
                    out_ref.at[head, part],
                    sem.at[len(copies)],
                )
            )
            copies[-1].start()
    for copy in copies:
        copy.wait()


def split_spatial(queries, keys, values):
    frames, spots, _ = queries.shape
    return pl.pallas_call(
        split_spatial_kernel,
        in_specs=[anywhere()] * 3,
        out_specs=whole(),
        out_shape=pltpu.VMEM((HS, 3, frames, spots, DH), BF16),
        scratch_shapes=[pltpu.SemaphoreType.DMA((HS * 3,))],
        compiler_params=params(),
        name="split_spatial",
    )(in_hbm(queries), in_hbm(keys), in_hbm(values))


def split_temporal_kernel(group_ref, q_ref, k_ref, v_ref, *rest):
    out_refs, sem = rest[:NF], rest[NF]
    group = group_ref[0]
    copies = []
    for slot in range(NF):
        at = pl.multiple_of((HS + lax.bitwise_xor(group, slot)) * DH, DH)
        for part, ref in enumerate((q_ref, k_ref, v_ref)):
            copies.append(
                pltpu.make_async_copy(
                    ref.at[:, :, pl.ds(at, DH)], out_refs[slot].at[part], sem.at[len(copies)]
                )
            )
            copies[-1].start()
    for copy in copies:
        copy.wait()


def split_temporal(group, queries, keys, values):
    frames, spots, _ = queries.shape
    return pl.pallas_call(
        split_temporal_kernel,
        in_specs=[scalars()] + [anywhere()] * 3,
        out_specs=[whole()] * NF,
        out_shape=[pltpu.VMEM((3, frames, spots, DH), BF16)] * NF,
        scratch_shapes=[pltpu.SemaphoreType.DMA((NF * 3,))],
        compiler_params=params(),
        name="split_temporal",
    )(group, in_hbm(queries), in_hbm(keys), in_hbm(values))


def collect_kernel(*refs):
    slabs, q_ref, kv_ref = refs[:NF], refs[NF], refs[NF + 1]
    per = q_ref.shape[0] // NF
    for slot in range(NF):
        at = slice(slot * per, (slot + 1) * per)
        q_ref[at] = slabs[slot][0].reshape(per, DH)
        kv_ref[0, at] = slabs[slot][1].reshape(per, DH)
        kv_ref[1, at] = slabs[slot][2].reshape(per, DH)


def collect(slabs):
    _, frames, spots, _ = slabs[0].shape
    rows = NF * frames * spots
    return pl.pallas_call(
        collect_kernel,
        in_specs=[whole()] * NF,
        out_specs=[whole()] * 2,
        out_shape=[pltpu.HBM((rows, DH), BF16), pltpu.VMEM((2, rows, DH), BF16)],
        compiler_params=params(),
        name="collect",
    )(*[in_vmem(slab) for slab in slabs])


def scores_of(q, k):
    return lax.dot_general(q, k, (((1,), (1,)), ((), ())), preferred_element_type=F32)


def with_ones(v):
    return jnp.concatenate([v, jnp.ones_like(v)], axis=1)


def temporal_kernel(offsets, resume, finish, *refs):
    count = len(offsets)
    strip_ref, q_ref = refs[:2]
    kv_refs = refs[2 : 2 + count]
    rest = list(refs[2 + count :])
    if resume:
        old_top, old_mix = rest[:2]
        rest = rest[2:]
    if finish:
        group_ref, out_ref = rest[:2]
        rest = rest[2:]
    top_ref, mix_ref, s_buf = rest[:3]
    rows = q_ref.shape[0]
    tiles = rows // QT
    own_strip = strip_ref[0]
    step = 1 - 2 * lax.rem(own_strip, 2)

    if resume:
        sem = rest[-1]
        loads = [
            pltpu.make_async_copy(old_top, top_ref, sem.at[0]),
            pltpu.make_async_copy(old_mix, mix_ref, sem.at[1]),
        ]
        for load in loads:
            load.start()
        for load in loads:
            load.wait()
    else:
        top_ref[...] = jnp.full(top_ref.shape, NEG_FILL, F32)
        mix_ref[...] = jnp.zeros(mix_ref.shape, F32)

    def attend(kv_ref):
        k = kv_ref[0]

        def q_tile(i):
            return q_ref[i * QT : (i + 1) * QT]

        s_buf[0] = scores_of(q_tile(0), k)
        for i in range(tiles):
            if i + 1 < tiles:
                s_buf[(i + 1) % 2] = scores_of(q_tile(i + 1), k)
            at = slice(i * QT, (i + 1) * QT)
            s = s_buf[i % 2]
            before = top_ref[at]
            top = jnp.maximum(before, jnp.max(s, axis=1, keepdims=True))
            fade = jnp.exp2((before - top) * RATE)
            weights = jnp.exp2((s - top[:, :1]) * RATE).astype(BF16)
            mixed = jnp.dot(weights, with_ones(kv_ref[1]), preferred_element_type=F32)
            mix_ref[at] = mixed + mix_ref[at] * jnp.concatenate([fade, fade], axis=1)
            top_ref[at] = top

    def usable(index):
        source = own_strip + offsets[index] * step
        return (source >= 0) & (source < NS)

    if count == 1:
        pl.when(usable(0))(lambda: attend(kv_refs[0]))
    else:
        kv_buf = rest[3]

        def strip(index, carry):
            valid = False
            for i in range(count):
                here = index == i

                @pl.when(here)
                def _(i=i):
                    kv_buf[...] = kv_refs[i][...]

                valid = valid | (here & usable(i))
            pl.when(valid)(lambda: attend(kv_buf))
            return carry

        lax.fori_loop(0, count, strip, 0)
    if finish:
        per = rows // NF
        for slot in range(NF):
            at = slice(slot * per, (slot + 1) * per)
            result = (mix_ref[at, :DH] / mix_ref[at, DH:]).astype(BF16)
            out_ref[lax.bitwise_xor(group_ref[0], slot)] = result.reshape(out_ref.shape[1:])


def temporal(strip, q, strips, state=None, keep=False, finish=None):
    rows = q.shape[0]
    count = len(strips)
    state_shape = [pltpu.VMEM((rows, DH), F32), pltpu.VMEM((rows, 2 * DH), F32)]
    args = [strip, in_hbm(q), *[in_vmem(x) for x in strips.values()]]
    in_specs = [scalars()] + [whole()] * (1 + count)
    scratch = [pltpu.VMEM((2, QT, rows), F32)]
    if count > 1:
        scratch.append(pltpu.VMEM((2, rows, DH), BF16))
    if state is not None:
        args += state
        in_specs += [anywhere()] * 2
        scratch.append(pltpu.SemaphoreType.DMA((2,)))
    if finish is not None:
        group, shape = finish
        args.append(group)
        in_specs.append(scalars())
        out_shape = [pltpu.HBM(shape, BF16)]
        scratch = state_shape + scratch
    elif keep:
        out_shape = state_shape
    else:
        out_shape = [pltpu.HBM(x.shape, x.dtype) for x in state_shape]
    cost = pl.CostEstimate(
        flops=count * rows**2 * DH * 8,
        transcendentals=count * rows**2,
        bytes_accessed=count * rows * DH * 4,
    )
    offsets = tuple(strips)
    return pl.pallas_call(
        lambda *refs: temporal_kernel(offsets, state is not None, finish is not None, *refs),
        in_specs=in_specs,
        out_specs=[whole()] * len(out_shape),
        out_shape=out_shape,
        scratch_shapes=scratch,
        compiler_params=params(20),
        cost_estimate=cost,
    )(*args)


def pick_kernel(strip_ref, pattern_ref, masks_ref, out_ref):
    pattern = pattern_ref[strip_ref[0]]
    blocks = out_ref.shape[0]
    for i in range(blocks):
        for j in range(blocks):
            out_ref[i, j] = masks_ref[pattern, i, j]


def pick(strip, head_pattern, masks):
    return pl.pallas_call(
        pick_kernel,
        in_specs=[scalars()] * 3,
        out_specs=scalars(),
        out_shape=jax.ShapeDtypeStruct(masks.shape[1:], masks.dtype),
        name="pick",
    )(strip, head_pattern, masks)


def spatial_kernel(mask_ref, qkv_ref, out_ref, s_buf, result_ref, sem):
    strips, frames, spots, _ = out_ref.shape
    positions = strips * spots
    blocks = positions // BLK
    tiles = positions // QS
    per = QS // spots

    def raw(f, i):
        q = qkv_ref[i * per : (i + 1) * per, 0, f].reshape(QS, DH)
        return scores_of(q, qkv_ref[:, 1, f].reshape(positions, DH))

    def masked(s, i):
        rows = []
        for r in range(QS // BLK):
            row = i * (QS // BLK) + r
            cells = []
            for j in range(blocks):
                bias = jnp.where(mask_ref[row, j] > 0, 0.0, NEG_FILL)
                cells.append(s[r * BLK : (r + 1) * BLK, j * BLK : (j + 1) * BLK] + bias)
            rows.append(jnp.concatenate(cells, axis=1))
        return jnp.concatenate(rows, axis=0)

    s_buf[0] = raw(0, 0)

    def frame(f, carry):
        v = with_ones(qkv_ref[:, 2, f].reshape(positions, DH))
        for i in range(tiles):
            if i + 1 < tiles:
                s_buf[(i + 1) % 2] = raw(f, i + 1)
            else:
                s_buf[(i + 1) % 2] = raw(jnp.minimum(f + 1, frames - 1), 0)
            s = masked(s_buf[i % 2], i)
            top = jnp.max(s, axis=1, keepdims=True)
            weights = jnp.exp2((s - top) * RATE).astype(BF16)
            mixed = jnp.dot(weights, v, preferred_element_type=F32)
            result = (mixed[:, :DH] / mixed[:, DH:]).astype(BF16)
            result_ref[f, i * per : (i + 1) * per] = result.reshape(per, spots, DH)
        leave(f).start()
        return carry

    def leave(f):
        return pltpu.make_async_copy(result_ref.at[f], out_ref.at[:, f], sem.at[f])

    lax.fori_loop(0, frames, frame, 0)
    for f in range(frames):
        leave(f).wait()


def spatial(mask, qkv):
    strips, _, frames, spots, _ = qkv.shape
    positions = strips * spots
    cost = pl.CostEstimate(
        flops=frames * positions**2 * DH * 8,
        transcendentals=frames * positions**2,
        bytes_accessed=4 * strips * frames * spots * DH * 2,
    )
    return pl.pallas_call(
        spatial_kernel,
        in_specs=[scalars(), whole()],
        out_specs=anywhere(),
        scratch_shapes=[
            pltpu.VMEM((2, QS, positions), F32),
            pltpu.VMEM((frames, strips, spots, DH), BF16),
            pltpu.SemaphoreType.DMA((frames,)),
        ],
        out_shape=pltpu.HBM((strips, frames, spots, DH), BF16),
        compiler_params=params(12),
        cost_estimate=cost,
        name="spatial",
    )(mask, in_vmem(qkv))


def join_kernel(first, heads_ref, *rest):
    out_ref, sem = rest[-2:]
    copies = []
    for head in range(heads_ref.shape[0]):
        at = (first + head) * DH
        copies.append(
            pltpu.make_async_copy(heads_ref.at[head], out_ref.at[:, :, at : at + DH], sem.at[head])
        )
        copies[-1].start()
    for copy in copies:
        copy.wait()


def join(heads, first, partial=None):
    count, frames, spots, _ = heads.shape
    args = [in_vmem(heads)]
    if partial is not None:
        args.append(partial)
    return pl.pallas_call(
        lambda *refs: join_kernel(first, *refs),
        in_specs=[whole(), anywhere()][: len(args)],
        out_specs=anywhere(),
        out_shape=jax.ShapeDtypeStruct((frames, spots, (HS + HT) * DH), BF16),
        scratch_shapes=[pltpu.SemaphoreType.DMA((count,))],
        input_output_aliases={} if partial is None else {1: 0},
        compiler_params=params(),
        name="join_spatial" if partial is None else "join_temporal",
    )(*args)


def paired(block, slot):
    return lax.ppermute(block, "frame", [(i, i ^ slot) for i in range(NF)])


def main(queries, keys, values, block_masks, head_pattern):
    frames, spots, _ = queries.shape
    group = lax.axis_index("frame").astype(jnp.int32)
    strip = lax.axis_index("strip").astype(jnp.int32)
    group_arg = group.reshape(1)
    strip_arg = strip.reshape(1)

    slabs = split_temporal(group_arg, queries, keys, values)
    slabs = [slabs[0]] + [paired(slabs[d], d) for d in range(1, NF)]
    qkv = split_spatial(queries, keys, values)
    qkv = lax.all_to_all(qkv, "strip", split_axis=0, concat_axis=0, tiled=True)
    mask = pick(strip_arg, head_pattern, block_masks)
    t_q, own = collect(slabs)

    swap = [(i, i ^ 1) for i in range(NS)]
    shared_from = [i + 2 if i % 2 == 0 else i - 2 for i in range(NS)]
    single_from = [i - 2 if i % 2 == 0 else i + 2 for i in range(NS)]
    partner = lax.ppermute(own, "strip", swap)
    shared = lax.ppermute(
        own, "strip", [(s, i) for i, s in enumerate(shared_from) if 0 <= s < NS]
    )
    own_later, shared = lax.optimization_barrier((own, shared))
    single = lax.ppermute(
        own_later, "strip", [(s, i) for i, s in enumerate(single_from) if 0 <= s < NS]
    )
    passed = lax.ppermute(shared, "strip", swap)

    state = temporal(strip_arg, t_q, {0: own, 1: partner})
    state = temporal(strip_arg, t_q, {2: shared, -1: passed}, [in_hbm(x) for x in state], keep=True)
    t_out = temporal(
        strip_arg,
        t_q,
        {-2: single},
        [in_vmem(x) for x in state],
        finish=(group_arg, (NF, frames, spots, DH)),
    )[0]
    t_out = lax.all_to_all(t_out, "frame", split_axis=0, concat_axis=0, tiled=True)
    s_out = spatial(mask, qkv)
    s_out = lax.all_to_all(s_out, "strip", split_axis=0, concat_axis=0, tiled=True)
    partial = join(s_out, 0)
    return join(t_out, HS, partial)


def solution(mesh):
    spec = P("frame", "strip", None)
    return jax.shard_map(
        main,
        mesh=mesh,
        in_specs=(spec, spec, spec, P(), P()),
        out_specs=spec,
        check_vma=False,
    )
```

```python
import functools
import math

import jax
import jax.numpy as jnp
from jax import lax
from jax.experimental import pallas as pl
from jax.experimental.pallas import tpu as pltpu
from jax.sharding import PartitionSpec as P


DH = 128
HS = 16
HT = 8
BLK = 128
NF = 8
NS = 16
QT = 512
QS = 256

NEG_FILL = -1e30
RATE = math.log2(math.e) / math.sqrt(DH)


BF16 = jnp.bfloat16
F32 = jnp.float32


def whole():
    return pl.BlockSpec(memory_space=pltpu.VMEM)


def scalars():
    return pl.BlockSpec(memory_space=pltpu.SMEM)


def anywhere():
    return pl.BlockSpec(memory_space=pl.ANY)


def in_vmem(block):
    return pltpu.with_memory_space_constraint(block, pltpu.VMEM)


def in_hbm(block):
    return pltpu.with_memory_space_constraint(block, pltpu.HBM)


def params(mib=8):
    return pltpu.CompilerParams(vmem_limit_bytes=mib * 1024 * 1024)


def load_parts(refs, frames, lanes, buf, sem):
    copies = [
        pltpu.make_async_copy(ref.at[frames, :, lanes], buf.at[part], sem.at[part])
        for part, ref in enumerate(refs)
    ]
    for copy in copies:
        copy.start()
    return copies


def split_spatial_kernel(first, q_ref, k_ref, v_ref, out_ref, buf, sem):
    frames = slice(first, first + out_ref.shape[2])
    copies = load_parts((q_ref, k_ref, v_ref), frames, slice(0, HS * DH), buf, sem)
    for part, copy in enumerate(copies):
        copy.wait()
        for head in range(HS):
            out_ref[head, part] = buf[part, :, :, head * DH : (head + 1) * DH]


def split_spatial(first, frames, queries, keys, values):
    spots = queries.shape[1]
    return pl.pallas_call(
        functools.partial(split_spatial_kernel, first),
        in_specs=[anywhere()] * 3,
        out_specs=whole(),
        out_shape=pltpu.HBM((HS, 3, frames, spots, DH), BF16),
        scratch_shapes=[
            pltpu.VMEM((3, frames, spots, HS * DH), BF16),
            pltpu.SemaphoreType.DMA((3,)),
        ],
        compiler_params=params(),
        name="split_spatial",
    )(in_hbm(queries), in_hbm(keys), in_hbm(values))


def split_temporal_kernel(group_ref, q_ref, k_ref, v_ref, *rest):
    out_refs, (buf, sem) = rest[:NF], rest[NF:]
    lanes = slice(HS * DH, (HS + HT) * DH)
    frames = slice(0, q_ref.shape[0])
    copies = load_parts((q_ref, k_ref, v_ref), frames, lanes, buf, sem)
    for part, copy in enumerate(copies):
        copy.wait()
        for slot in range(NF):
            at = pl.multiple_of(lax.bitwise_xor(group_ref[0], slot) * DH, DH)
            out_refs[slot][part] = buf[part, :, :, pl.ds(at, DH)]


def split_temporal(group, queries, keys, values):
    frames, spots, _ = queries.shape
    return pl.pallas_call(
        split_temporal_kernel,
        in_specs=[scalars()] + [anywhere()] * 3,
        out_specs=[whole()] * NF,
        out_shape=[pltpu.VMEM((3, frames, spots, DH), BF16)] * NF,
        scratch_shapes=[
            pltpu.VMEM((3, frames, spots, HT * DH), BF16),
            pltpu.SemaphoreType.DMA((3,)),
        ],
        compiler_params=params(),
        name="split_temporal",
    )(group, in_hbm(queries), in_hbm(keys), in_hbm(values))


def collect_kernel(*refs):
    slabs, q_ref, kv_ref = refs[:NF], refs[NF], refs[NF + 1]
    per = q_ref.shape[0] // NF
    for slot in range(NF):
        at = slice(slot * per, (slot + 1) * per)
        q_ref[at] = slabs[slot][0].reshape(per, DH)
        kv_ref[0, at] = slabs[slot][1].reshape(per, DH)
        kv_ref[1, at] = slabs[slot][2].reshape(per, DH)


def collect(slabs):
    _, frames, spots, _ = slabs[0].shape
    rows = NF * frames * spots
    return pl.pallas_call(
        collect_kernel,
        in_specs=[whole()] * NF,
        out_specs=[whole()] * 2,
        out_shape=[pltpu.HBM((rows, DH), BF16), pltpu.VMEM((2, rows, DH), BF16)],
        compiler_params=params(),
        name="collect",
    )(*[in_vmem(slab) for slab in slabs])


def scores_of(q, k):
    return lax.dot_general(q, k, (((1,), (1,)), ((), ())), preferred_element_type=F32)


def with_ones(v):
    return jnp.concatenate([v, jnp.ones_like(v)], axis=1)


def usable(strip_ref, offset):
    source = strip_ref[0] + offset * (1 - 2 * lax.rem(strip_ref[0], 2))
    return (source >= 0) & (source < NS)


def attend(q_ref, kv_ref, s_buf, state, done):
    k = kv_ref[0]
    tiles = q_ref.shape[0] // QT

    def raw(i):
        return scores_of(q_ref[i * QT : (i + 1) * QT], k)

    s_buf[0] = raw(0)
    for i in range(tiles):
        if i + 1 < tiles:
            s_buf[(i + 1) % 2] = raw(i + 1)
        at = slice(i * QT, (i + 1) * QT)
        s = s_buf[i % 2]
        top = jnp.broadcast_to(jnp.max(s, axis=1, keepdims=True), (QT, DH))
        if state is not None:
            before = state[0][at]
            top = jnp.maximum(before, top)
            fade = jnp.exp2((before - top) * RATE)
        weights = jnp.exp2((s - top[:, :1]) * RATE).astype(BF16)
        mixed = jnp.dot(weights, with_ones(kv_ref[1]), preferred_element_type=F32)
        if state is not None:
            mixed = mixed + state[1][at] * jnp.concatenate([fade, fade], axis=1)
        done(i, top, mixed)


def temporal_kernel(offsets, resume, strip_ref, q_ref, *refs):
    count = len(offsets)
    kv_refs, rest = refs[:count], refs[count:]
    if resume:
        old_top, old_mix, top_ref, mix_ref, s_buf, sem = rest
        loads = [
            pltpu.make_async_copy(old_top, top_ref, sem.at[0]),
            pltpu.make_async_copy(old_mix, mix_ref, sem.at[1]),
        ]
        for load in loads:
            load.start()
        for load in loads:
            load.wait()
    else:
        top_ref, mix_ref, s_buf = rest

    def done(i, top, mixed):
        at = slice(i * QT, (i + 1) * QT)
        top_ref[at] = top
        mix_ref[at] = mixed

    for offset, kv_ref in zip(offsets, kv_refs):
        if offset == 0:
            attend(q_ref, kv_ref, s_buf, None, done)
        else:
            pl.when(usable(strip_ref, offset))(
                lambda kv_ref=kv_ref: attend(q_ref, kv_ref, s_buf, (top_ref, mix_ref), done)
            )


def temporal(strip, q, strips, state=None):
    rows = q.shape[0]
    count = len(strips)
    state_shape = [((rows, DH), F32), ((rows, 2 * DH), F32)]
    args = [strip, in_hbm(q), *[in_vmem(x) for x in strips.values()]]
    in_specs = [scalars()] + [whole()] * (1 + count)
    scratch = [pltpu.VMEM((2, QT, rows), F32)]
    if state is not None:
        args += [in_hbm(x) for x in state]
        in_specs += [anywhere()] * 2
        scratch.append(pltpu.SemaphoreType.DMA((2,)))
    space = pltpu.HBM if state is None else pltpu.VMEM
    cost = pl.CostEstimate(
        flops=count * rows**2 * DH * 8,
        transcendentals=count * rows**2,
        bytes_accessed=count * rows * DH * 4,
    )
    return pl.pallas_call(
        functools.partial(temporal_kernel, tuple(strips), state is not None),
        in_specs=in_specs,
        out_specs=[whole()] * 2,
        out_shape=[space(*shape) for shape in state_shape],
        scratch_shapes=scratch,
        compiler_params=params(20),
        cost_estimate=cost,
    )(*args)


def temporal_last_kernel(offset, strip_ref, group_ref, q_ref, kv_ref, top_ref, mix_ref, *rest):
    out_ref, s_buf = rest
    per = q_ref.shape[0] // NF
    slots = QT // per

    def done(i, _, mixed):
        for r in range(slots):
            rows = mixed[r * per : (r + 1) * per]
            result = (rows[:, :DH] / rows[:, DH:]).astype(BF16)
            target = lax.bitwise_xor(group_ref[0], i * slots + r)
            out_ref[target] = result.reshape(out_ref.shape[1:])

    valid = usable(strip_ref, offset)
    pl.when(valid)(lambda: attend(q_ref, kv_ref, s_buf, (top_ref, mix_ref), done))

    @pl.when(jnp.logical_not(valid))
    def _():
        for i in range(NF // slots):
            done(i, None, mix_ref[i * QT : (i + 1) * QT])


def temporal_last(strip, group, q, offset, kv, state, shape):
    rows = q.shape[0]
    return pl.pallas_call(
        functools.partial(temporal_last_kernel, offset),
        in_specs=[scalars()] * 2 + [whole()] * 4,
        out_specs=whole(),
        out_shape=pltpu.HBM(shape, BF16),
        scratch_shapes=[pltpu.VMEM((2, QT, rows), F32)],
        compiler_params=params(20),
        cost_estimate=pl.CostEstimate(
            flops=rows**2 * DH * 8, transcendentals=rows**2, bytes_accessed=rows * DH * 4
        ),
        name="temporal_last",
    )(strip, group, in_hbm(q), *[in_vmem(x) for x in (kv, *state)])


def spatial_kernel(first, strip_ref, pattern_ref, mask_ref, qkv_ref, *rest):
    pattern = pattern_ref[strip_ref[0]]
    out_ref, s_buf, result_ref, sem = rest[-4:]
    frames, strips, spots, _ = result_ref.shape
    positions = strips * spots
    blocks = positions // BLK
    tiles = positions // QS
    per = QS // spots

    def raw(f, i):
        q = qkv_ref[i * per : (i + 1) * per, 0, f].reshape(QS, DH)
        return scores_of(q, qkv_ref[:, 1, f].reshape(positions, DH))

    def masked(s, i):
        rows = []
        for r in range(QS // BLK):
            row = i * (QS // BLK) + r
            cells = []
            for j in range(blocks):
                bias = jnp.where(mask_ref[pattern, row, j] > 0, 0.0, NEG_FILL)
                cells.append(s[r * BLK : (r + 1) * BLK, j * BLK : (j + 1) * BLK] + bias)
            rows.append(jnp.concatenate(cells, axis=1))
        return jnp.concatenate(rows, axis=0)

    s_buf[0] = raw(0, 0)

    def frame(f, carry):
        v = with_ones(qkv_ref[:, 2, f].reshape(positions, DH))
        for i in range(tiles):
            if i + 1 < tiles:
                s_buf[(i + 1) % 2] = raw(f, i + 1)
            else:
                s_buf[(i + 1) % 2] = raw(jnp.minimum(f + 1, frames - 1), 0)
            s = masked(s_buf[i % 2], i)
            top = jnp.max(s, axis=1, keepdims=True)
            weights = jnp.exp2((s - top) * RATE).astype(BF16)
            mixed = jnp.dot(weights, v, preferred_element_type=F32)
            result = (mixed[:, :DH] / mixed[:, DH:]).astype(BF16)
            result_ref[f, i * per : (i + 1) * per] = result.reshape(per, spots, DH)
        leave(f).start()
        return carry

    def leave(f):
        return pltpu.make_async_copy(result_ref.at[f], out_ref.at[:, first + f], sem.at[f])

    lax.fori_loop(0, frames, frame, 0)
    for f in range(frames):
        leave(f).wait()


def spatial(first, frames_all, strip, head_pattern, masks, qkv, partial=None):
    strips, _, frames, spots, _ = qkv.shape
    positions = strips * spots
    cost = pl.CostEstimate(
        flops=frames * positions**2 * DH * 8,
        transcendentals=frames * positions**2,
        bytes_accessed=4 * strips * frames * spots * DH * 2,
    )
    args = [strip, head_pattern, masks, in_vmem(qkv)]
    if partial is not None:
        args.append(in_hbm(partial))
    return pl.pallas_call(
        functools.partial(spatial_kernel, first),
        in_specs=[*[scalars()] * 3, whole(), anywhere()][: len(args)],
        out_specs=anywhere(),
        scratch_shapes=[
            pltpu.VMEM((2, QS, positions), F32),
            pltpu.VMEM((frames, strips, spots, DH), BF16),
            pltpu.SemaphoreType.DMA((frames,)),
        ],
        out_shape=pltpu.HBM((strips, frames_all, spots, DH), BF16),
        input_output_aliases={} if partial is None else {4: 0},
        compiler_params=params(12),
        cost_estimate=cost,
        name="spatial",
    )(*args)


def join_kernel(first, heads_ref, *rest):
    out_ref, sem = rest[-2:]
    copies = []
    for head in range(heads_ref.shape[0]):
        at = (first + head) * DH
        copies.append(
            pltpu.make_async_copy(heads_ref.at[head], out_ref.at[:, :, at : at + DH], sem.at[head])
        )
        copies[-1].start()
    for copy in copies:
        copy.wait()


def join(heads, first, partial=None):
    count, frames, spots, _ = heads.shape
    args = [in_vmem(heads)]
    if partial is not None:
        args.append(partial)
    return pl.pallas_call(
        lambda *refs: join_kernel(first, *refs),
        in_specs=[whole(), anywhere()][: len(args)],
        out_specs=anywhere(),
        out_shape=jax.ShapeDtypeStruct((frames, spots, (HS + HT) * DH), BF16),
        scratch_shapes=[pltpu.SemaphoreType.DMA((count,))],
        input_output_aliases={} if partial is None else {1: 0},
        compiler_params=params(),
        name="join_spatial" if partial is None else "join_temporal",
    )(*args)


def paired(block, slot):
    return lax.ppermute(block, "frame", [(i, i ^ slot) for i in range(NF)])


def main(queries, keys, values, block_masks, head_pattern):
    frames, spots, _ = queries.shape
    group = lax.axis_index("frame").astype(jnp.int32)
    strip = lax.axis_index("strip").astype(jnp.int32)
    group_arg = group.reshape(1)
    strip_arg = strip.reshape(1)

    half = frames // 2
    qkv_a = split_spatial(0, half, queries, keys, values)
    qkv_a = lax.all_to_all(qkv_a, "strip", split_axis=0, concat_axis=0, tiled=True)
    slabs = split_temporal(group_arg, queries, keys, values)
    slabs = [slabs[0]] + [paired(slabs[d], d) for d in range(1, NF)]
    qkv_b = split_spatial(half, half, queries, keys, values)
    qkv_b = lax.all_to_all(qkv_b, "strip", split_axis=0, concat_axis=0, tiled=True)
    t_q, own = collect(slabs)

    swap = [(i, i ^ 1) for i in range(NS)]
    shared_from = [i + 2 if i % 2 == 0 else i - 2 for i in range(NS)]
    single_from = [i - 2 if i % 2 == 0 else i + 2 for i in range(NS)]
    partner = lax.ppermute(own, "strip", swap)
    shared = lax.ppermute(own, "strip", [(s, i) for i, s in enumerate(shared_from) if 0 <= s < NS])
    own_later, shared = lax.optimization_barrier((own, shared))
    single = lax.ppermute(
        own_later, "strip", [(s, i) for i, s in enumerate(single_from) if 0 <= s < NS]
    )
    passed = lax.ppermute(shared, "strip", swap)

    state = temporal(strip_arg, t_q, {0: own, 1: partner})
    state = temporal(strip_arg, t_q, {2: shared, -1: passed}, state)
    t_out = temporal_last(
        strip_arg, group_arg, t_q, -2, single, state, (NF, frames, spots, DH)
    )
    t_out = lax.all_to_all(t_out, "frame", split_axis=0, concat_axis=0, tiled=True)
    s_out = spatial(0, frames, strip_arg, head_pattern, block_masks, qkv_a)
    s_out = spatial(half, frames, strip_arg, head_pattern, block_masks, qkv_b, s_out)
    s_out = lax.all_to_all(s_out, "strip", split_axis=0, concat_axis=0, tiled=True)
    partial = join(s_out, 0)
    return join(t_out, HS, partial)


def solution(mesh):
    spec = P("frame", "strip", None)
    return jax.shard_map(
        main,
        mesh=mesh,
        in_specs=(spec, spec, spec, P(), P()),
        out_specs=spec,
        check_vma=False,
    )
```

```python
import functools
import math

import jax
import jax.numpy as jnp
from jax import lax
from jax.experimental import pallas as pl
from jax.experimental.pallas import tpu as pltpu
from jax.sharding import PartitionSpec as P


DH = 128
HS = 16
HT = 8
BLK = 128
NF = 8
NS = 16
QT = 512
QS = 256

NEG_FILL = -1e30
RATE = math.log2(math.e) / math.sqrt(DH)


BF16 = jnp.bfloat16
F32 = jnp.float32


def whole():
    return pl.BlockSpec(memory_space=pltpu.VMEM)


def scalars():
    return pl.BlockSpec(memory_space=pltpu.SMEM)


def anywhere():
    return pl.BlockSpec(memory_space=pl.ANY)


def in_vmem(block):
    return pltpu.with_memory_space_constraint(block, pltpu.VMEM)


def in_hbm(block):
    return pltpu.with_memory_space_constraint(block, pltpu.HBM)


def params(mib=8):
    return pltpu.CompilerParams(vmem_limit_bytes=mib * 1024 * 1024)


def load_parts(refs, frames, lanes, buf, sem):
    copies = [
        pltpu.make_async_copy(ref.at[frames, :, lanes], buf.at[part], sem.at[part])
        for part, ref in enumerate(refs)
    ]
    for copy in copies:
        copy.start()
    return copies


def split_spatial_kernel(first, q_ref, k_ref, v_ref, out_ref, buf, sem):
    frames = slice(first, first + out_ref.shape[2])
    copies = load_parts((q_ref, k_ref, v_ref), frames, slice(0, HS * DH), buf, sem)
    for part, copy in enumerate(copies):
        copy.wait()
        for head in range(HS):
            out_ref[head, part] = buf[part, :, :, head * DH : (head + 1) * DH]


def split_spatial(first, frames, queries, keys, values):
    spots = queries.shape[1]
    return pl.pallas_call(
        functools.partial(split_spatial_kernel, first),
        in_specs=[anywhere()] * 3,
        out_specs=whole(),
        out_shape=pltpu.HBM((HS, 3, frames, spots, DH), BF16),
        scratch_shapes=[
            pltpu.VMEM((3, frames, spots, HS * DH), BF16),
            pltpu.SemaphoreType.DMA((3,)),
        ],
        compiler_params=params(),
        name="split_spatial",
    )(in_hbm(queries), in_hbm(keys), in_hbm(values))


def split_temporal_kernel(group_ref, q_ref, k_ref, v_ref, *rest):
    out_refs, (buf, sem) = rest[:NF], rest[NF:]
    lanes = slice(HS * DH, (HS + HT) * DH)
    frames = slice(0, q_ref.shape[0])
    copies = load_parts((q_ref, k_ref, v_ref), frames, lanes, buf, sem)
    for part, copy in enumerate(copies):
        copy.wait()
        for slot in range(NF):
            at = pl.multiple_of(lax.bitwise_xor(group_ref[0], slot) * DH, DH)
            out_refs[slot][part] = buf[part, :, :, pl.ds(at, DH)]


def split_temporal(group, queries, keys, values):
    frames, spots, _ = queries.shape
    return pl.pallas_call(
        split_temporal_kernel,
        in_specs=[scalars()] + [anywhere()] * 3,
        out_specs=[whole()] * NF,
        out_shape=[pltpu.VMEM((3, frames, spots, DH), BF16)] * NF,
        scratch_shapes=[
            pltpu.VMEM((3, frames, spots, HT * DH), BF16),
            pltpu.SemaphoreType.DMA((3,)),
        ],
        compiler_params=params(),
        name="split_temporal",
    )(group, in_hbm(queries), in_hbm(keys), in_hbm(values))


def collect_kernel(*refs):
    slabs, q_ref, kv_ref = refs[:NF], refs[NF], refs[NF + 1]
    per = q_ref.shape[0] // NF
    for slot in range(NF):
        at = slice(slot * per, (slot + 1) * per)
        q_ref[at] = slabs[slot][0].reshape(per, DH)
        kv_ref[0, at] = slabs[slot][1].reshape(per, DH)
        kv_ref[1, at] = slabs[slot][2].reshape(per, DH)


def collect(slabs):
    _, frames, spots, _ = slabs[0].shape
    rows = NF * frames * spots
    return pl.pallas_call(
        collect_kernel,
        in_specs=[whole()] * NF,
        out_specs=[whole()] * 2,
        out_shape=[pltpu.HBM((rows, DH), BF16), pltpu.VMEM((2, rows, DH), BF16)],
        compiler_params=params(),
        name="collect",
    )(*[in_vmem(slab) for slab in slabs])


def scores_of(q, k):
    return lax.dot_general(q, k, (((1,), (1,)), ((), ())), preferred_element_type=F32)


def with_ones(v):
    return jnp.concatenate([v, jnp.ones_like(v)], axis=1)


def usable(strip_ref, offset):
    source = strip_ref[0] + offset * (1 - 2 * lax.rem(strip_ref[0], 2))
    return (source >= 0) & (source < NS)


def attend(q_ref, kv_ref, s_buf, state, ready, done):
    k = kv_ref[0]
    tiles = q_ref.shape[0] // QT

    def raw(i):
        return scores_of(q_ref[i * QT : (i + 1) * QT], k)

    s_buf[0] = raw(0)
    ready()
    for i in range(tiles):
        if i + 1 < tiles:
            s_buf[(i + 1) % 2] = raw(i + 1)
        at = slice(i * QT, (i + 1) * QT)
        s = s_buf[i % 2]
        top = jnp.broadcast_to(jnp.max(s, axis=1, keepdims=True), (QT, DH))
        if state is not None:
            before = state[0][at]
            top = jnp.maximum(before, top)
            fade = jnp.exp2((before - top) * RATE)
        weights = jnp.exp2((s - top[:, :1]) * RATE).astype(BF16)
        mixed = jnp.dot(weights, with_ones(kv_ref[1]), preferred_element_type=F32)
        if state is not None:
            mixed = mixed + state[1][at] * jnp.concatenate([fade, fade], axis=1)
        done(i, top, mixed)


def state_copies(sources, targets, sem, tile=None):
    at = slice(0, sources[0].shape[0]) if tile is None else slice(tile * QT, (tile + 1) * QT)
    first = 0 if tile is None else 2 * tile
    return [
        pltpu.make_async_copy(source.at[at], target.at[at], sem.at[first + n])
        for n, (source, target) in enumerate(zip(sources, targets))
    ]


def first_kernel(q_ref, own_ref, partner_ref, top_out, mix_out, s_buf, top_ref, mix_ref, sem):
    tiles = q_ref.shape[0] // QT
    state = (top_ref, mix_ref)

    def leave(i):
        return state_copies(state, (top_out, mix_out), sem, i)

    def keep(i, top, mixed):
        at = slice(i * QT, (i + 1) * QT)
        top_ref[at] = top
        mix_ref[at] = mixed

    def send(i, top, mixed):
        keep(i, top, mixed)
        for copy in leave(i):
            copy.start()

    attend(q_ref, own_ref, s_buf, None, lambda: None, keep)
    attend(q_ref, partner_ref, s_buf, state, lambda: None, send)
    for i in range(tiles):
        for copy in leave(i):
            copy.wait()


def state_shapes(rows):
    return [((rows, DH), F32), ((rows, 2 * DH), F32)]


def temporal_cost(count, rows):
    return pl.CostEstimate(
        flops=count * rows**2 * DH * 8,
        transcendentals=count * rows**2,
        bytes_accessed=count * rows * DH * 4,
    )


def temporal_first(q, own, partner):
    rows = q.shape[0]
    shapes = state_shapes(rows)
    return pl.pallas_call(
        first_kernel,
        in_specs=[whole()] * 3,
        out_specs=[anywhere()] * 2,
        out_shape=[pltpu.HBM(*shape) for shape in shapes],
        scratch_shapes=[
            pltpu.VMEM((2, QT, rows), F32),
            *[pltpu.VMEM(*shape) for shape in shapes],
            pltpu.SemaphoreType.DMA((2 * (rows // QT),)),
        ],
        compiler_params=params(24),
        cost_estimate=temporal_cost(2, rows),
        name="temporal_first",
    )(in_hbm(q), in_vmem(own), in_vmem(partner))


def middle_kernel(offsets, strip_ref, q_ref, *refs):
    count = len(offsets)
    kv_refs, (old_top, old_mix, top_ref, mix_ref, s_buf, kv_buf, sem) = refs[:count], refs[count:]
    loads = state_copies((old_top, old_mix), (top_ref, mix_ref), sem)
    for load in loads:
        load.start()

    def arrive():
        for load in loads:
            load.wait()

    def done(i, top, mixed):
        at = slice(i * QT, (i + 1) * QT)
        top_ref[at] = top
        mix_ref[at] = mixed

    def strip(index, carry):
        valid = False
        for i in range(count):
            here = index == i

            @pl.when(here)
            def _(i=i):
                kv_buf[...] = kv_refs[i][...]

            valid = valid | (here & usable(strip_ref, offsets[i]))

        def ready():
            pl.when(index == 0)(arrive)

        pl.when(valid)(lambda: attend(q_ref, kv_buf, s_buf, (top_ref, mix_ref), ready, done))
        pl.when((index == 0) & jnp.logical_not(valid))(arrive)
        return carry

    lax.fori_loop(0, count, strip, 0)


def temporal_middle(strip, q, strips, state):
    rows = q.shape[0]
    count = len(strips)
    return pl.pallas_call(
        functools.partial(middle_kernel, tuple(strips)),
        in_specs=[scalars(), *[whole()] * (1 + count), *[anywhere()] * 2],
        out_specs=[whole()] * 2,
        out_shape=[pltpu.VMEM(*shape) for shape in state_shapes(rows)],
        scratch_shapes=[
            pltpu.VMEM((2, QT, rows), F32),
            pltpu.VMEM((2, rows, DH), BF16),
            pltpu.SemaphoreType.DMA((2,)),
        ],
        compiler_params=params(20),
        cost_estimate=temporal_cost(count, rows),
        name="temporal_middle",
    )(strip, in_hbm(q), *[in_vmem(x) for x in strips.values()], *[in_hbm(x) for x in state])


def temporal_last_kernel(offset, strip_ref, group_ref, q_ref, kv_ref, top_ref, mix_ref, *rest):
    out_ref, s_buf = rest
    per = q_ref.shape[0] // NF
    slots = QT // per

    def done(i, _, mixed):
        for r in range(slots):
            rows = mixed[r * per : (r + 1) * per]
            result = (rows[:, :DH] / rows[:, DH:]).astype(BF16)
            target = lax.bitwise_xor(group_ref[0], i * slots + r)
            out_ref[target] = result.reshape(out_ref.shape[1:])

    valid = usable(strip_ref, offset)
    pl.when(valid)(
        lambda: attend(q_ref, kv_ref, s_buf, (top_ref, mix_ref), lambda: None, done)
    )

    @pl.when(jnp.logical_not(valid))
    def _():
        for i in range(NF // slots):
            done(i, None, mix_ref[i * QT : (i + 1) * QT])


def temporal_last(strip, group, q, offset, kv, state, shape):
    rows = q.shape[0]
    return pl.pallas_call(
        functools.partial(temporal_last_kernel, offset),
        in_specs=[scalars()] * 2 + [whole()] * 4,
        out_specs=whole(),
        out_shape=pltpu.HBM(shape, BF16),
        scratch_shapes=[pltpu.VMEM((2, QT, rows), F32)],
        compiler_params=params(20),
        cost_estimate=temporal_cost(1, rows),
        name="temporal_last",
    )(strip, group, in_hbm(q), *[in_vmem(x) for x in (kv, *state)])


def spatial_kernel(first, strip_ref, pattern_ref, mask_ref, qkv_ref, *rest):
    pattern = pattern_ref[strip_ref[0]]
    out_ref, s_buf, result_ref, sem = rest[-4:]
    frames, strips, spots, _ = result_ref.shape
    positions = strips * spots
    blocks = positions // BLK
    tiles = positions // QS
    per = QS // spots

    def raw(f, i):
        q = qkv_ref[i * per : (i + 1) * per, 0, f].reshape(QS, DH)
        return scores_of(q, qkv_ref[:, 1, f].reshape(positions, DH))

    def masked(s, i):
        rows = []
        for r in range(QS // BLK):
            row = i * (QS // BLK) + r
            cells = []
            for j in range(blocks):
                bias = jnp.where(mask_ref[pattern, row, j] > 0, 0.0, NEG_FILL)
                cells.append(s[r * BLK : (r + 1) * BLK, j * BLK : (j + 1) * BLK] + bias)
            rows.append(jnp.concatenate(cells, axis=1))
        return jnp.concatenate(rows, axis=0)

    s_buf[0] = raw(0, 0)

    def frame(f, carry):
        v = with_ones(qkv_ref[:, 2, f].reshape(positions, DH))
        for i in range(tiles):
            if i + 1 < tiles:
                s_buf[(i + 1) % 2] = raw(f, i + 1)
            else:
                s_buf[(i + 1) % 2] = raw(jnp.minimum(f + 1, frames - 1), 0)
            s = masked(s_buf[i % 2], i)
            top = jnp.max(s, axis=1, keepdims=True)
            weights = jnp.exp2((s - top) * RATE).astype(BF16)
            mixed = jnp.dot(weights, v, preferred_element_type=F32)
            result = (mixed[:, :DH] / mixed[:, DH:]).astype(BF16)
            result_ref[f, i * per : (i + 1) * per] = result.reshape(per, spots, DH)
        leave(f).start()
        return carry

    def leave(f):
        return pltpu.make_async_copy(result_ref.at[f], out_ref.at[:, first + f], sem.at[f])

    lax.fori_loop(0, frames, frame, 0)
    for f in range(frames):
        leave(f).wait()


def spatial(first, frames_all, strip, head_pattern, masks, qkv, partial=None):
    strips, _, frames, spots, _ = qkv.shape
    positions = strips * spots
    cost = pl.CostEstimate(
        flops=frames * positions**2 * DH * 8,
        transcendentals=frames * positions**2,
        bytes_accessed=4 * strips * frames * spots * DH * 2,
    )
    args = [strip, head_pattern, masks, in_vmem(qkv)]
    if partial is not None:
        args.append(in_hbm(partial))
    return pl.pallas_call(
        functools.partial(spatial_kernel, first),
        in_specs=[*[scalars()] * 3, whole(), anywhere()][: len(args)],
        out_specs=anywhere(),
        scratch_shapes=[
            pltpu.VMEM((2, QS, positions), F32),
            pltpu.VMEM((frames, strips, spots, DH), BF16),
            pltpu.SemaphoreType.DMA((frames,)),
        ],
        out_shape=pltpu.HBM((strips, frames_all, spots, DH), BF16),
        input_output_aliases={} if partial is None else {4: 0},
        compiler_params=params(12),
        cost_estimate=cost,
        name="spatial",
    )(*args)


def join_kernel(first, heads_ref, *rest):
    out_ref, sem = rest[-2:]
    copies = []
    for head in range(heads_ref.shape[0]):
        at = (first + head) * DH
        copies.append(
            pltpu.make_async_copy(heads_ref.at[head], out_ref.at[:, :, at : at + DH], sem.at[head])
        )
        copies[-1].start()
    for copy in copies:
        copy.wait()


def join(heads, first, partial=None):
    count, frames, spots, _ = heads.shape
    args = [in_vmem(heads)]
    if partial is not None:
        args.append(partial)
    return pl.pallas_call(
        lambda *refs: join_kernel(first, *refs),
        in_specs=[whole(), anywhere()][: len(args)],
        out_specs=anywhere(),
        out_shape=jax.ShapeDtypeStruct((frames, spots, (HS + HT) * DH), BF16),
        scratch_shapes=[pltpu.SemaphoreType.DMA((count,))],
        input_output_aliases={} if partial is None else {1: 0},
        compiler_params=params(),
        name="join_spatial" if partial is None else "join_temporal",
    )(*args)


def paired(block, slot):
    return lax.ppermute(block, "frame", [(i, i ^ slot) for i in range(NF)])


def main(queries, keys, values, block_masks, head_pattern):
    frames, spots, _ = queries.shape
    group = lax.axis_index("frame").astype(jnp.int32)
    strip = lax.axis_index("strip").astype(jnp.int32)
    group_arg = group.reshape(1)
    strip_arg = strip.reshape(1)

    half = frames // 2
    qkv_a = split_spatial(0, half, queries, keys, values)
    qkv_a = lax.all_to_all(qkv_a, "strip", split_axis=0, concat_axis=0, tiled=True)
    slabs = split_temporal(group_arg, queries, keys, values)
    moved = {0: slabs[0]}
    moved.update({d: paired(slabs[d], d) for d in range(1, NF, 2)})
    moved.update({d: paired(slabs[d], d) for d in range(2, NF, 2)})
    slabs = [moved[d] for d in range(NF)]
    qkv_b = split_spatial(half, half, queries, keys, values)
    qkv_b = lax.all_to_all(qkv_b, "strip", split_axis=0, concat_axis=0, tiled=True)
    t_q, own = collect(slabs)

    swap = [(i, i ^ 1) for i in range(NS)]
    shared_from = [i + 2 if i % 2 == 0 else i - 2 for i in range(NS)]
    single_from = [i - 2 if i % 2 == 0 else i + 2 for i in range(NS)]
    partner = lax.ppermute(own, "strip", swap)
    shared = lax.ppermute(own, "strip", [(s, i) for i, s in enumerate(shared_from) if 0 <= s < NS])
    own_later, shared = lax.optimization_barrier((own, shared))
    single = lax.ppermute(
        own_later, "strip", [(s, i) for i, s in enumerate(single_from) if 0 <= s < NS]
    )
    passed = lax.ppermute(shared, "strip", swap)

    state = temporal_first(t_q, own, partner)
    state = temporal_middle(strip_arg, t_q, {2: shared, -1: passed}, state)
    t_out = temporal_last(
        strip_arg, group_arg, t_q, -2, single, state, (NF, frames, spots, DH)
    )
    t_out = lax.all_to_all(t_out, "frame", split_axis=0, concat_axis=0, tiled=True)
    s_out = spatial(0, frames, strip_arg, head_pattern, block_masks, qkv_a)
    s_out = spatial(half, frames, strip_arg, head_pattern, block_masks, qkv_b, s_out)
    s_out = lax.all_to_all(s_out, "strip", split_axis=0, concat_axis=0, tiled=True)
    partial = join(s_out, 0)
    return join(t_out, HS, partial)


def solution(mesh):
    spec = P("frame", "strip", None)
    return jax.shard_map(
        main,
        mesh=mesh,
        in_specs=(spec, spec, spec, P(), P()),
        out_specs=spec,
        check_vma=False,
    )
```
